256 devices in a mesh: gx: 16 (over z_lo, x), gy: 4 (over z_hi, core), gz: 4 (over y).
Axes of the slice: x: 4, y: 4, z: 8 (z_hi: 2, z_lo: 4; z = z_hi * 4 + z_lo), core: 2. Of those that a mesh axis runs over, the one named last changes fastest.
Arguments:
- inverse_blocks: bfloat16 [50, 50, 98304], P(None, None, ('gx', 'gy', 'gz')), may hold values from -0.875 to 0.875
- face_blocks: bfloat16 [4, 50, 50, 98304], P(None, None, None, ('gx', 'gy', 'gz')), may hold values from -0.4375 to 0.4375
- load_vector: bfloat16 [50, 8, 98304], P(None, None, ('gx', 'gy', 'gz')), may hold values from -6 to 6
- live_counts: int32 [256], P(('gx', 'gy', 'gz')), may hold values from 192 to 384, as said below
- nbr_kind: int32 [4, 98304], P(None, ('gx', 'gy', 'gz')), may hold values from 0 to 7, as said below
- nbr_slot: int32 [4, 98304], P(None, ('gx', 'gy', 'gz')), may hold values from 0 to 383, as said below
- send_x: int32 [256, 2, 128], P(('gx', 'gy', 'gz')), may hold values from 0 to 383, as said below
- send_yz: int32 [256, 4, 64], P(('gx', 'gy', 'gz')), may hold values from 0 to 383, as said below
Outputs:
- adjoint: bfloat16 [50, 8, 98304], P(None, None, ('gx', 'gy', 'gz'))
The draws below stay inside these ranges and needn't reach their ends.
Inputs may be any that keep to these rules, and one draw needn't show every extreme that they name: Device d has live_counts[d] live elements, at least 192; some device has 384. `nbr_kind`: 0 means no neighbour, 1 a neighbour on the same device, 2 + j a neighbour received from direction j; a direction whose source device does not exist is never named; faces of slots that are not live are 0. `nbr_slot`: for kind 1 a live element of the same device; for kinds 2 and 3 below 128; for kinds 4 to 7 below 64; 0 for kind 0. `send_x`: live elements of the sending device; the entries of one device's list for one direction are distinct. `send_yz`: live elements of the sending device; the entries of one device's list for one direction are distinct.
All inputs are finite; a program needn't handle non-finite values.
Results may differ from the reference program's by a relative error of at most 0.012.
Values may be sent and summed in bfloat16 or wider, within the bound.
A program may use at most 128 MiB of HBM per device.

```python
import jax
import jax.numpy as jnp

NB = 50
NF = 8
FACES = 4
SWEEPS = 2
E_DEV = 384
HALO_X = 128
HALO_YZ = 64
ELEMS = 98304
N_GX = 16
N_GY = 4
N_GZ = 4
DEVICES = 256


def layout(key):
    counts = jax.random.randint(jax.random.fold_in(key, 11), (DEVICES,), E_DEV // 2, E_DEV + 1)
    chosen = jax.random.randint(jax.random.fold_in(key, 12), (), 0, DEVICES)
    counts = counts.at[chosen].set(E_DEV)
    device = jnp.arange(DEVICES, dtype=jnp.int32)
    coord_list = [device // (N_GY * N_GZ), device // N_GZ % N_GY, device % N_GZ]
    extent_list = [N_GX, N_GY, N_GZ]
    exist_list = []
    for direction in range(6):
        axis_number = direction // 2
        step_by = 1 - 2 * (direction % 2)
        moved = coord_list[axis_number] - step_by
        exist_list.append((moved >= 0) & (moved < extent_list[axis_number]))
    exists = jnp.stack(exist_list, axis=1)
    shape = (FACES, DEVICES, E_DEV)
    chance = jax.random.randint(jax.random.fold_in(key, 13), shape, 0, 100)
    pick_dir = jax.random.randint(jax.random.fold_in(key, 14), shape, 0, 8)
    direction = jnp.where(pick_dir < 4, pick_dir // 2, pick_dir - 2)
    reach = exists[device[None, :, None], direction]
    kind = jnp.where(chance < 5, 0, jnp.where((chance < 50) & reach, direction + 2, 1))
    living = jnp.arange(E_DEV)[None, None, :] < counts[None, :, None]
    kind = jnp.where(living, kind, 0)
    return (counts, kind)


def send_lists(key, salt, rows, width):
    counts = layout(key)[0]
    shape = (DEVICES, rows, E_DEV)
    noise = jax.random.randint(jax.random.fold_in(key, salt), shape, 0, 2 ** 20)
    index = jnp.arange(E_DEV, dtype=jnp.int32)[None, None, :]
    dead = index >= counts[:, None, None]
    score = noise * E_DEV + index + jnp.where(dead, 2 ** 30, 0)
    order = jnp.argsort(score, axis=2, stable=True)
    return order[:, :, :width].astype(jnp.int32)


def draw_live_counts(key, part):
    return layout(key)[0].astype(jnp.int32)


def draw_nbr_kind(key, part):
    return layout(key)[1].reshape(FACES, DEVICES * E_DEV).astype(jnp.int32)


def draw_nbr_slot(key, part):
    counts, kind = layout(key)
    shape = (FACES, DEVICES, E_DEV)
    local_slot = jax.random.randint(jax.random.fold_in(key, 15), shape, 0, counts[None, :, None])
    bound = jnp.where(kind >= 4, HALO_YZ, HALO_X)
    remote_slot = jax.random.randint(jax.random.fold_in(key, 16), shape, 0, bound)
    slot_value = jnp.where(kind == 1, local_slot, jnp.where(kind >= 2, remote_slot, 0))
    return slot_value.reshape(FACES, DEVICES * E_DEV).astype(jnp.int32)


def draw_send_x(key, part):
    return send_lists(key, 17, 2, HALO_X)


def draw_send_yz(key, part):
    return send_lists(key, 18, 4, HALO_YZ)


def steps_of(stream_key, shape, shards, smallest, largest):
    def one(axis_at, blocks):
        draws = jax.random.uniform(jax.random.fold_in(jax.random.fold_in(stream_key, 6), axis_at), (blocks,), jnp.float32, smallest / len(shards), largest / len(shards))
        return jnp.repeat(jnp.exp(draws), shape[axis_at] // blocks).reshape((-1,) + (1,) * (len(shape) - axis_at - 1))

    level = one(*shards[0])
    for cut in shards[1:]:
        level = level * one(*cut)
    return level


def normal_values(rng, extent, deviation, limit, cuts=(), kind=jnp.bfloat16):
    array = deviation * jax.random.normal(rng, extent, jnp.float32)
    if cuts:
        array = array * steps_of(rng, extent, cuts, -0.22, 0.18)
    return jnp.clip(array, -limit, limit).astype(kind)


def setup_inputs(seed: int = 0) -> dict:
    keys = jax.random.split(jax.random.key(seed), 9)
    return {
        "inverse_blocks": normal_values(keys[0], (NB, NB, ELEMS), NB ** -0.5, 0.875, ((2, 256),)),
        "face_blocks": normal_values(keys[1], (FACES, NB, NB, ELEMS), (4 * NB) ** -0.5, 0.4375, ((3, 256),)),
        "load_vector": normal_values(keys[2], (NB, NF, ELEMS), 1.0, 6.0, ((2, 256),)),
        "live_counts": draw_live_counts(jax.random.fold_in(keys[8], 71), 0),
        "nbr_kind": draw_nbr_kind(jax.random.fold_in(keys[8], 71), 0),
        "nbr_slot": draw_nbr_slot(jax.random.fold_in(keys[8], 71), 0),
        "send_x": draw_send_x(jax.random.fold_in(keys[8], 71), 0),
        "send_yz": draw_send_yz(jax.random.fold_in(keys[8], 71), 0),
    }


def neighbours(nbr_kind, nbr_slot, send_x, send_yz):
    elements = nbr_kind.shape[1]
    device = (jnp.arange(elements, dtype=jnp.int32) // E_DEV).astype(jnp.int32)
    coord_list = [device // (N_GY * N_GZ), (device // N_GZ) % N_GY, device % N_GZ]
    extent_list = [N_GX, N_GY, N_GZ]
    global_index = device[None, :] * E_DEV + nbr_slot
    for direction in range(6):
        axis_number = direction // 2
        step_by = 1 - 2 * (direction % 2)
        moved = list(coord_list)
        moved[axis_number] = jnp.clip(coord_list[axis_number] - step_by, 0, extent_list[axis_number] - 1)
        source = ((moved[0] * N_GY + moved[1]) * N_GZ + moved[2]).astype(jnp.int32)
        if direction < 2:
            slot_index = jnp.clip(nbr_slot, 0, HALO_X - 1)
            local_index = send_x[source[None, :], direction, slot_index]
        else:
            slot_index = jnp.clip(nbr_slot, 0, HALO_YZ - 1)
            local_index = send_yz[source[None, :], direction - 2, slot_index]
        global_index = jnp.where(nbr_kind == direction + 2, source[None, :] * E_DEV + local_index, global_index)
    return jnp.where(nbr_kind == 0, 0, global_index).astype(jnp.int32)


def block_apply(blocks, vectors):
    return jnp.einsum("ije,jke->ike", blocks.astype(jnp.float32), vectors.astype(jnp.float32))


def reference(inverse_blocks, face_blocks, load_vector, live_counts, nbr_kind, nbr_slot, send_x, send_yz):
    elements = load_vector.shape[2]
    positions = jnp.arange(elements, dtype=jnp.int32)
    live_mask = (positions % E_DEV) < live_counts[positions // E_DEV]
    global_index = neighbours(nbr_kind, nbr_slot, send_x, send_yz)
    active = nbr_kind > 0
    adjoint = jnp.where(live_mask, block_apply(inverse_blocks, load_vector), 0.0).astype(jnp.bfloat16)
    for repeat in range(SWEEPS):
        coupling = jnp.zeros(load_vector.shape, jnp.float32)
        for face in range(FACES):
            beside = jnp.where(active[face], adjoint[:, :, global_index[face]], jnp.zeros((), jnp.bfloat16))
            coupling = coupling + block_apply(face_blocks[face], beside)
        residual = (load_vector.astype(jnp.float32) - coupling).astype(jnp.bfloat16)
        adjoint = jnp.where(live_mask, block_apply(inverse_blocks, residual), 0.0).astype(jnp.bfloat16)
    return adjoint
```

```python
import jax
import jax.numpy as jnp
from jax import lax
from jax.experimental import pallas as pl
from jax.experimental.pallas import tpu as pltpu
from jax.sharding import PartitionSpec as P

BF = jnp.bfloat16
F32 = jnp.float32
I32 = jnp.int32
SWEEPS = 2
NB = 50
NF = 8
FACES = 4
ROWS = NB * NF
E = 384
L = 128
T = E // L
FR = 208
XR = 64
HALO = 512
SRC = E + HALO
PACK = 208
DIRECTIONS = (("gx", 1), ("gx", -1), ("gy", 1), ("gy", -1), ("gz", 1), ("gz", -1))
OFFSETS = (0, E, E + 128, E + 256, E + 320, E + 384, E + 448)
MESH = pl.DeviceIdType.MESH
FACE_GROUPS = ((0, 1, 2, 3), (4, 5, 6), (7, 8, 9), (10, 11, 12))
INV_GROUPS = ((0, 1, 2, 3),)


def at16(index):
    return pl.ds(pl.multiple_of(index * 16, 16), 16)


def whole_tiles(get, count):
    value = jnp.concatenate([get(m) for m in range(count)], axis=0)
    return [value[16 * m : 16 * m + 16] for m in range(count)]


def kernel(
    inv_hbm, face_hbm, load_ref, live_ref, kind_ref, slot_ref, sx_ref, syz_ref, out_ref,
    faces, inverse, adj, wide_x, vec_x, wide_b, vec_b, pick_send, pick, send_x, send_yz, recv_x, recv_yz,
    block_sem, send_sem, recv_sem,
):
    position = {axis: lax.axis_index(axis) for axis in ("gx", "gy", "gz")}
    sends, receives = [], []
    for axis, step in DIRECTIONS:
        length = lax.axis_size(axis)
        ahead, behind = position[axis] + step, position[axis] - step
        sends.append((ahead >= 0) & (ahead < length))
        receives.append((behind >= 0) & (behind < length))

    def block_copy(t):
        return pltpu.make_async_copy(
            inv_hbm.at[:, :, pl.ds(L * t, L)], inverse.at[t, :, pl.ds(0, NB), :], block_sem.at[t]
        )

    def face_copy(t):
        return pltpu.make_async_copy(
            face_hbm.reshape(NB, NB * FACES, E).at[:, :, pl.ds(L * t, L)],
            faces.at[t, :, pl.ds(0, NB * FACES), :],
            block_sem.at[T + t],
        )

    for t in range(T):
        block_copy(t).start()
    for t in range(T):
        face_copy(t).start()

    for d in range(6):

        @pl.when(jnp.logical_not(receives[d]))
        def _(d=d):
            for s in range(SWEEPS):
                if d < 2:
                    recv_x[s, d] = jnp.zeros((ROWS, L), BF)
                else:
                    recv_yz[s, d - 2] = jnp.zeros((PACK, L), BF)

    barrier = pltpu.get_barrier_semaphore()
    for d, (axis, step) in enumerate(DIRECTIONS):

        @pl.when(sends[d])
        def _(axis=axis, step=step):
            pl.semaphore_signal(
                barrier, inc=1, device_id={axis: position[axis] + step}, device_id_type=MESH
            )

    def halo_copy(s, d):
        axis, step = DIRECTIONS[d]
        source, target = (send_x, recv_x) if d < 2 else (send_yz, recv_yz)
        at = d if d < 2 else d - 2
        beside = jnp.clip(position[axis] + step, 0, lax.axis_size(axis) - 1)
        return pltpu.make_async_remote_copy(
            src_ref=source.at[s, at],
            dst_ref=target.at[s, at],
            send_sem=send_sem.at[s, d],
            recv_sem=recv_sem.at[s, d],
            device_id={axis: beside},
            device_id_type=MESH,
        )

    live = live_ref[0]
    lane = lax.broadcasted_iota(I32, (16, L), 1)
    low = lane < 64
    group_sum = (
        lax.shift_right_logical(lax.broadcasted_iota(I32, (16, 256), 1), 4)
        == lax.broadcasted_iota(I32, (16, 256), 0)
    )
    group_sum = group_sum.astype(F32).astype(BF)

    def pad_tile(t, _):
        for k in range(NF):
            wide_x[t, k * XR + 48 : k * XR + 64, :] = jnp.zeros((16, L), F32)
            wide_b[t, k * FR + 200 : k * FR + 208, :] = jnp.zeros((8, L), F32)

        def pad_row(i, _):
            faces[t, i, 200:208, :] = jnp.zeros((8, L), BF)
            return 0

        return lax.fori_loop(0, NB, pad_row, 0)

    lax.fori_loop(0, T, pad_tile, 0)

    def lanes(t):
        return pl.ds(pl.multiple_of(t * L, L), L)

    def scatter_x(t, i2, value):
        for half in range(2):
            wide_x[t, pl.ds(2 * i2 + half, NF, stride=XR), :] = value[8 * half : 8 * half + 8]

    def narrow_x(t):
        for k in range(NF):
            for m in range(XR // 16):
                r = k * XR + 16 * m
                vec_x[t, k, 16 * m : 16 * m + 16, :] = wide_x[t, r : r + 16, :].astype(BF)

    def contract(blocks, vectors, count, groups):
        tiles = [whole_tiles(lambda m, half=half: blocks(half, m), count) for half in range(2)]
        sums = {}
        for k in range(NF):
            vector = whole_tiles(lambda m, k=k: vectors(k, m), count)
            for g, members in enumerate(groups):
                for half in range(2):
                    total = None
                    for m in members:
                        product = tiles[half][m] * vector[m]
                        total = product if total is None else total + product
                    sums[g, half, k] = total
        stacked = [
            sums[g, half, k] for g in range(len(groups)) for half in range(2) for k in range(NF)
        ]
        return jnp.dot(
            jnp.concatenate([group_sum] * len(groups), axis=1),
            jnp.concatenate(stacked, axis=0),
            preferred_element_type=F32,
        )

    def load_rows(t, i2):
        return load_ref[at16(i2), lanes(t)].astype(F32)

    def apply_inverse(t, s):
        alive = (lane + t * L) < live

        def body(i2, _):
            total = contract(
                lambda half, m: inverse[t, 2 * i2 + half, 16 * m : 16 * m + 16, :],
                lambda k, m: vec_x[t, k, 16 * m : 16 * m + 16, :],
                XR // 16,
                INV_GROUPS,
            )
            adj[s, at16(i2), lanes(t)] = jnp.where(alive, total, 0.0).astype(BF)
            return 0

        lax.fori_loop(0, NB // 2, body, 0, unroll=5)

    def apply_faces(t):
        def body(i2, _):
            total = contract(
                lambda half, m: faces[t, 2 * i2 + half, 16 * m : 16 * m + 16, :],
                lambda k, m: vec_b[t, k, 16 * m : 16 * m + 16, :],
                FR // 16,
                FACE_GROUPS,
            )
            scatter_x(t, i2, load_rows(t, i2) - total)
            return 0

        lax.fori_loop(0, NB // 2, body, 0, unroll=5)

    lists = [sx_ref[0, 0:1, :], sx_ref[0, 1:2, :]]
    for pair in range(2):
        lists.append(
            jnp.concatenate(
                [syz_ref[0, 2 * pair : 2 * pair + 1, :], syz_ref[0, 2 * pair + 1 : 2 * pair + 2, :]],
                axis=1,
            )
        )
    for c in range(4):

        def fill_send(b, _, c=c):
            row = lax.broadcasted_iota(I32, (16, L), 0) + b * 16
            pick_send[at16(b), c * L : (c + 1) * L] = jnp.where(row == lists[c], 1.0, 0.0).astype(BF)
            return 0

        lax.fori_loop(0, E // 16, fill_send, 0, unroll=8)

    def load_tile(i2, _):
        for t in range(T):
            scatter_x(t, i2, load_rows(t, i2))
        return 0

    lax.fori_loop(0, NB // 2, load_tile, 0)
    for t in range(T):
        block_copy(t).wait()

    def first(t, _):
        def clear(i, _):
            tail = inverse[t, i, 48:64, :].astype(F32)
            row = lax.broadcasted_iota(I32, (16, L), 0)
            inverse[t, i, 48:64, :] = jnp.where(row < 2, tail, 0.0).astype(BF)
            return 0

        lax.fori_loop(0, NB, clear, 0, unroll=5)
        narrow_x(t)
        apply_inverse(t, 0)
        return 0

    lax.fori_loop(0, T, first, 0)

    def send_halo(s):
        for pair in (0, 1):
            both = jnp.dot(
                adj[s, :, 0:E], pick_send[:, (2 + pair) * L : (3 + pair) * L], preferred_element_type=F32
            )
            for r in range(PACK // 16):
                upper = both[16 * r : 16 * r + 16]
                if PACK + 16 * r < ROWS:
                    lower = both[PACK + 16 * r : PACK + 16 * r + 16]
                else:
                    lower = jnp.zeros((16, L), F32)
                ahead = jnp.where(low, upper, pltpu.roll(lower, 64, 1))
                behind = jnp.where(low, pltpu.roll(upper, 64, 1), lower)
                send_yz[s, 2 * pair, 16 * r : 16 * r + 16, :] = ahead.astype(BF)
                send_yz[s, 2 * pair + 1, 16 * r : 16 * r + 16, :] = behind.astype(BF)
            if pair == 0:
                start_halo(s, (2, 3))
                for d in range(2):
                    send_x[s, d] = jnp.dot(
                        adj[s, :, 0:E], pick_send[:, d * L : (d + 1) * L], preferred_element_type=F32
                    ).astype(BF)
                start_halo(s, (0, 1))
        start_halo(s, (4, 5))

    def start_halo(s, directions):
        for d in directions:

            @pl.when(sends[d])
            def _(d=d):
                halo_copy(s, d).start()

    def take_halo(s):
        for d in range(6):

            @pl.when(receives[d])
            def _(d=d):
                halo_copy(s, d).wait_recv()

        for d in range(2):
            adj[s, :, E + d * L : E + (d + 1) * L] = recv_x[s, d]
        for pair in range(2):
            column = E + (2 + pair) * L
            for r in range(PACK // 16):
                ahead = recv_yz[s, 2 * pair, 16 * r : 16 * r + 16, :].astype(F32)
                behind = recv_yz[s, 2 * pair + 1, 16 * r : 16 * r + 16, :].astype(F32)
                upper = jnp.where(low, ahead, pltpu.roll(behind, 64, 1))
                adj[s, 16 * r : 16 * r + 16, column : column + L] = upper.astype(BF)
                if PACK + 16 * r < ROWS:
                    lower = jnp.where(low, pltpu.roll(ahead, 64, 1), behind)
                    adj[s, PACK + 16 * r : PACK + 16 * r + 16, column : column + L] = lower.astype(BF)

    def gather_faces(t, s):
        for f in range(0, FACES, 2):
            picked = jnp.dot(adj[s], pick[t, :, f * L : (f + 2) * L], preferred_element_type=F32)
            for j in range(NB):
                for g in range(2):
                    rows = pl.ds(FACES * j + f + g, NF, stride=FR)
                    wide_b[t, rows, :] = picked[8 * j : 8 * j + 8, g * L : (g + 1) * L]

        def narrow(k, _):
            for m in range(FR // 16):
                r = pl.ds(pl.multiple_of(k * FR + 16 * m, 16), 16)
                vec_b[t, k, 16 * m : 16 * m + 16, :] = wide_b[t, r, :].astype(BF)
            return 0

        lax.fori_loop(0, NF, narrow, 0)

    pl.semaphore_wait(barrier, sum(jnp.where(there, 1, 0) for there in sends))
    send_halo(0)

    kind = kind_ref[...]
    look = jnp.where(kind == 0, -1, slot_ref[...])
    for d in range(7):
        look = look + jnp.where(kind == d + 1, OFFSETS[d], 0)
    for t in range(T):
        for f in range(FACES):
            wanted = look[f : f + 1, t * L : (t + 1) * L]

            def fill(b, _, t=t, f=f, wanted=wanted):
                row = lax.broadcasted_iota(I32, (16, L), 0) + b * 16
                pick[t, at16(b), f * L : (f + 1) * L] = jnp.where(row == wanted, 1.0, 0.0).astype(BF)
                return 0

            lax.fori_loop(0, SRC // 16, fill, 0, unroll=8)
    for t in range(T):
        face_copy(t).wait()

    for s in range(SWEEPS):
        take_halo(s)

        def sweep(t, _, s=s):
            gather_faces(t, s)
            apply_faces(t)
            narrow_x(t)
            apply_inverse(t, s + 1)
            return 0

        lax.fori_loop(0, T, sweep, 0)
        if s + 1 < SWEEPS:
            send_halo(s + 1)
    out_ref[...] = adj[SWEEPS, :, 0:E]
    for s in range(SWEEPS):
        for d in range(6):

            @pl.when(sends[d])
            def _(s=s, d=d):
                halo_copy(s, d).wait_send()


def shards(inverse_blocks, face_blocks, load_vector, live_counts, nbr_kind, nbr_slot, send_x, send_yz):
    by_row = jnp.transpose(face_blocks, (1, 2, 0, 3))
    anywhere = pl.BlockSpec(memory_space=pl.ANY)
    on_core = pl.BlockSpec(memory_space=pltpu.VMEM)
    scalar = pl.BlockSpec(memory_space=pltpu.SMEM)
    result = pl.pallas_call(
        kernel,
        out_shape=jax.ShapeDtypeStruct((ROWS, E), BF),
        in_specs=[anywhere, anywhere, on_core, scalar, on_core, on_core, on_core, on_core],
        out_specs=on_core,
        scratch_shapes=[
            pltpu.VMEM((T, NB, FR, L), BF),
            pltpu.VMEM((T, NB, XR, L), BF),
            pltpu.VMEM((SWEEPS + 1, ROWS, SRC), BF),
            pltpu.VMEM((T, NF * XR, L), F32),
            pltpu.VMEM((T, NF, XR, L), BF),
            pltpu.VMEM((T, NF * FR, L), F32),
            pltpu.VMEM((T, NF, FR, L), BF),
            pltpu.VMEM((E, HALO), BF),
            pltpu.VMEM((T, SRC, FACES * L), BF),
            pltpu.VMEM((SWEEPS, 2, ROWS, L), BF),
            pltpu.VMEM((SWEEPS, 4, PACK, L), BF),
            pltpu.VMEM((SWEEPS, 2, ROWS, L), BF),
            pltpu.VMEM((SWEEPS, 4, PACK, L), BF),
            pltpu.SemaphoreType.DMA((2 * T,)),
            pltpu.SemaphoreType.DMA((SWEEPS, 6)),
            pltpu.SemaphoreType.DMA((SWEEPS, 6)),
        ],
        compiler_params=pltpu.CompilerParams(
            vmem_limit_bytes=60 * 2**20, collective_id=0, has_side_effects=True
        ),
    )(
        inverse_blocks, by_row, load_vector.reshape(ROWS, E), live_counts,
        nbr_kind, nbr_slot, send_x, send_yz,
    )
    return result.reshape(NB, NF, E)


def solution(mesh):
    elements = ("gx", "gy", "gz")
    placed = (
        P(None, None, elements),
        P(None, None, None, elements),
        P(None, None, elements),
        P(elements),
        P(None, elements),
        P(None, elements),
        P(elements, None, None),
        P(elements, None, None),
    )
    return jax.shard_map(
        shards, mesh=mesh, in_specs=placed, out_specs=P(None, None, elements), check_vma=False
    )
```

```python
import jax
import jax.numpy as jnp
from jax import lax
from jax.experimental import pallas as pl
from jax.experimental.pallas import tpu as pltpu
from jax.sharding import PartitionSpec as P

BF = jnp.bfloat16
F32 = jnp.float32
I32 = jnp.int32
SWEEPS = 2
NB = 50
NF = 8
FACES = 4
ROWS = NB * NF
E = 384
L = 128
T = E // L
FR = 208
FS = 216
XR = 56
XS = 72
HALO = 512
SRC = E + HALO
PACK = 208
DIRECTIONS = (("gx", 1), ("gx", -1), ("gy", 1), ("gy", -1), ("gz", 1), ("gz", -1))
OFFSETS = (0, E, E + 128, E + 256, E + 320, E + 384, E + 448)
MESH = pl.DeviceIdType.MESH
FACE_GROUPS = ((0, 1, 2), (3, 4, 5), (6, 7, 8), (9, 10, 11, 12))


def at16(index):
    return pl.ds(pl.multiple_of(index * 16, 16), 16)


def whole_tiles(get, count):
    value = jnp.concatenate([get(m) for m in range(count)], axis=0)
    return [value[16 * m : 16 * m + 16] for m in range(count)]


def added(terms):
    total = None
    for term in terms:
        total = term if total is None else total + term
    return total


def kernel(
    inv_hbm, face_hbm, load_ref, live_ref, kind_ref, slot_ref, sx_ref, syz_ref, out_ref,
    faces, inverse, adj, wide_x, vec_x, wide_b, vec_b, pick_send, pick, send_x, send_yz, recv_x, recv_yz,
    block_sem, send_sem, recv_sem,
):
    position = {axis: lax.axis_index(axis) for axis in ("gx", "gy", "gz")}
    sends, receives = [], []
    for axis, step in DIRECTIONS:
        length = lax.axis_size(axis)
        ahead, behind = position[axis] + step, position[axis] - step
        sends.append((ahead >= 0) & (ahead < length))
        receives.append((behind >= 0) & (behind < length))

    def block_copy(t, h):
        return pltpu.make_async_copy(
            inv_hbm.at[:, h, :, pl.ds(L * t, L)],
            inverse.at[t, :, pl.ds(XR * h, NB), :],
            block_sem.at[2 * t + h],
        )

    def face_copy(t):
        return pltpu.make_async_copy(
            face_hbm.reshape(NB, NB * FACES, E).at[:, :, pl.ds(L * t, L)],
            faces.at[t, :, pl.ds(0, NB * FACES), :],
            block_sem.at[2 * T + t],
        )

    def pad_row(i, _):
        for t in range(T):
            for h in range(2):
                inverse[t, i, XR * h + NB : XR * h + XR, :] = jnp.zeros((XR - NB, L), BF)
                faces[t, 2 * i + h, 200:208, :] = jnp.zeros((8, L), BF)
        return 0

    for t in range(T):
        for h in range(2):
            block_copy(t, h).start()
    for t in range(T):
        face_copy(t).start()

    lax.fori_loop(0, NB // 2, pad_row, 0, unroll=5)
    for t in range(T):
        for k in range(NF):
            wide_x[t, k * XS + 48 : k * XS + 56, :] = jnp.zeros((8, L), F32)
            wide_b[t, k * FS + 200 : k * FS + 208, :] = jnp.zeros((8, L), F32)

    for d in range(6):

        @pl.when(jnp.logical_not(receives[d]))
        def _(d=d):
            for s in range(SWEEPS):
                if d < 2:
                    recv_x[s, d] = jnp.zeros((ROWS, L), BF)
                else:
                    recv_yz[s, d - 2] = jnp.zeros((PACK, L), BF)

    barrier = pltpu.get_barrier_semaphore()
    for d, (axis, step) in enumerate(DIRECTIONS):

        @pl.when(sends[d])
        def _(axis=axis, step=step):
            pl.semaphore_signal(
                barrier, inc=1, device_id={axis: position[axis] + step}, device_id_type=MESH
            )

    def halo_copy(s, d):
        axis, step = DIRECTIONS[d]
        source, target = (send_x, recv_x) if d < 2 else (send_yz, recv_yz)
        at = d if d < 2 else d - 2
        beside = jnp.clip(position[axis] + step, 0, lax.axis_size(axis) - 1)
        return pltpu.make_async_remote_copy(
            src_ref=source.at[s, at],
            dst_ref=target.at[s, at],
            send_sem=send_sem.at[s, d],
            recv_sem=recv_sem.at[s, d],
            device_id={axis: beside},
            device_id_type=MESH,
        )

    live = live_ref[0]
    lane = lax.broadcasted_iota(I32, (16, L), 1)
    low = lane < 64
    group_sum = (
        lax.shift_right_logical(lax.broadcasted_iota(I32, (16, 256), 1), 4)
        == lax.broadcasted_iota(I32, (16, 256), 0)
    )
    group_sum = group_sum.astype(F32).astype(BF)
    column = lax.broadcasted_iota(I32, (16, L), 1)
    split_sum = (
        lax.shift_right_logical(column, 4) + (column & 8) == lax.broadcasted_iota(I32, (16, L), 0)
    )
    split_sum = split_sum.astype(F32).astype(BF)

    def lanes(t):
        return pl.ds(pl.multiple_of(t * L, L), L)

    def scatter_x(t, i2, value):
        for half in range(2):
            wide_x[t, pl.ds(2 * i2 + half, NF, stride=XS), :] = value[8 * half : 8 * half + 8]

    def narrow_x(t):
        for k in range(NF):
            for m in range(2 * XR // 16):
                first = k * XS + (16 * m) % XR
                second = k * XS + (16 * m + 8) % XR
                both = jnp.concatenate(
                    [wide_x[t, first : first + 8, :], wide_x[t, second : second + 8, :]], axis=0
                )
                vec_x[t, k, 16 * m : 16 * m + 16, :] = both.astype(BF)

    def contract_faces(t, i2):
        count = FR // 16
        tiles = [
            whole_tiles(lambda m, h=h: faces[t, 2 * i2 + h, 16 * m : 16 * m + 16, :], count)
            for h in range(2)
        ]
        sums = {}
        for k in range(NF):
            vector = whole_tiles(lambda m, k=k: vec_b[t, k, 16 * m : 16 * m + 16, :], count)
            for g, members in enumerate(FACE_GROUPS):
                for h in range(2):
                    sums[g, h, k] = added(tiles[h][m] * vector[m] for m in members)
        stacked = [
            sums[g, h, k] for g in range(len(FACE_GROUPS)) for h in range(2) for k in range(NF)
        ]
        return jnp.dot(
            jnp.concatenate([group_sum] * len(FACE_GROUPS), axis=1),
            jnp.concatenate(stacked, axis=0),
            preferred_element_type=F32,
        )

    def contract_inverse(t, i2):
        count = 2 * XR // 16
        tiles = whole_tiles(lambda m: inverse[t, i2, 16 * m : 16 * m + 16, :], count)
        sums = {}
        for k in range(NF):
            vector = whole_tiles(lambda m, k=k: vec_x[t, k, 16 * m : 16 * m + 16, :], count)
            products = [tiles[m] * vector[m] for m in range(count)]
            sums[0, k] = added(products[:3])
            sums[1, k] = added(products[4:])
            sums[2, k] = products[3]
        return jnp.dot(
            jnp.concatenate([group_sum, split_sum], axis=1),
            jnp.concatenate([sums[part, k] for part in range(3) for k in range(NF)], axis=0),
            preferred_element_type=F32,
        )

    def load_rows(t, i2):
        return load_ref[at16(i2), lanes(t)].astype(F32)

    def apply_inverse(t, s):
        alive = (lane + t * L) < live

        for i2 in range(NB // 2):
            total = contract_inverse(t, i2)
            adj[s, 16 * i2 : 16 * i2 + 16, lanes(t)] = jnp.where(alive, total, 0.0).astype(BF)

    def apply_faces(t):
        for i2 in range(NB // 2):
            total = contract_faces(t, i2)
            scatter_x(t, i2, load_rows(t, i2) - total)

    lists = [sx_ref[0, 0:1, :], sx_ref[0, 1:2, :]]
    for pair in range(2):
        lists.append(
            jnp.concatenate(
                [syz_ref[0, 2 * pair : 2 * pair + 1, :], syz_ref[0, 2 * pair + 1 : 2 * pair + 2, :]],
                axis=1,
            )
        )
    for c in range(4):

        def fill_send(b, _, c=c):
            row = lax.broadcasted_iota(I32, (16, L), 0) + b * 16
            pick_send[at16(b), c * L : (c + 1) * L] = jnp.where(row == lists[c], 1.0, 0.0).astype(BF)
            return 0

        lax.fori_loop(0, E // 16, fill_send, 0, unroll=8)

    for i2 in range(NB // 2):
        for t in range(T):
            scatter_x(t, i2, load_rows(t, i2))
    for t in range(T):
        for h in range(2):
            block_copy(t, h).wait()

    def first(t, _):
        narrow_x(t)
        apply_inverse(t, 0)
        return 0

    lax.fori_loop(0, T, first, 0)

    def send_halo(s):
        four = jnp.dot(adj[s, :, 0:E], pick_send[:, 2 * L : 4 * L], preferred_element_type=F32)
        for pair in (0, 1):
            both = four[:, pair * L : (pair + 1) * L]
            for r in range(PACK // 16):
                upper = both[16 * r : 16 * r + 16]
                if PACK + 16 * r < ROWS:
                    lower = both[PACK + 16 * r : PACK + 16 * r + 16]
                else:
                    lower = jnp.zeros((16, L), F32)
                ahead = jnp.where(low, upper, pltpu.roll(lower, 64, 1))
                behind = jnp.where(low, pltpu.roll(upper, 64, 1), lower)
                send_yz[s, 2 * pair, 16 * r : 16 * r + 16, :] = ahead.astype(BF)
                send_yz[s, 2 * pair + 1, 16 * r : 16 * r + 16, :] = behind.astype(BF)
        start_halo(s, (2, 3, 4, 5))
        two = jnp.dot(adj[s, :, 0:E], pick_send[:, 0 : 2 * L], preferred_element_type=F32).astype(BF)
        for d in range(2):
            send_x[s, d] = two[:, d * L : (d + 1) * L]
        start_halo(s, (0, 1))

    def start_halo(s, directions):
        for d in directions:

            @pl.when(sends[d])
            def _(d=d):
                halo_copy(s, d).start()

    def take_halo(s):
        for d in range(6):

            @pl.when(receives[d])
            def _(d=d):
                halo_copy(s, d).wait_recv()

        for d in range(2):
            adj[s, :, E + d * L : E + (d + 1) * L] = recv_x[s, d]
        for pair in range(2):
            column = E + (2 + pair) * L
            for r in range(PACK // 16):
                ahead = recv_yz[s, 2 * pair, 16 * r : 16 * r + 16, :].astype(F32)
                behind = recv_yz[s, 2 * pair + 1, 16 * r : 16 * r + 16, :].astype(F32)
                upper = jnp.where(low, ahead, pltpu.roll(behind, 64, 1))
                adj[s, 16 * r : 16 * r + 16, column : column + L] = upper.astype(BF)
                if PACK + 16 * r < ROWS:
                    lower = jnp.where(low, pltpu.roll(ahead, 64, 1), behind)
                    adj[s, PACK + 16 * r : PACK + 16 * r + 16, column : column + L] = lower.astype(BF)

    def gather_rows(t, s):
        for f in range(0, FACES, 2):
            picked = jnp.dot(
                adj[s], pick[t, :, f * L : (f + 2) * L], preferred_element_type=F32
            )
            for j in range(NB):
                for g in range(2):
                    rows = pl.ds(FACES * j + f + g, NF, stride=FS)
                    wide_b[t, rows, :] = picked[8 * j : 8 * j + 8, g * L : (g + 1) * L]

    def narrow_b(t):
        for k in range(NF):
            for m in range(FR // 16):
                r = k * FS + 16 * m
                vec_b[t, k, 16 * m : 16 * m + 16, :] = wide_b[t, r : r + 16, :].astype(BF)

    pl.semaphore_wait(barrier, sum(jnp.where(there, 1, 0) for there in sends))
    send_halo(0)

    kind = kind_ref[...]
    look = jnp.where(kind == 0, -1, slot_ref[...])
    for d in range(7):
        look = look + jnp.where(kind == d + 1, OFFSETS[d], 0)
    for t in range(T):
        for f in range(FACES):
            wanted = look[f : f + 1, t * L : (t + 1) * L]

            def fill(b, _, t=t, f=f, wanted=wanted):
                row = lax.broadcasted_iota(I32, (16, L), 0) + b * 16
                pick[t, at16(b), f * L : (f + 1) * L] = jnp.where(row == wanted, 1.0, 0.0).astype(BF)
                return 0

            lax.fori_loop(0, SRC // 16, fill, 0, unroll=8)
    for t in range(T):
        face_copy(t).wait()

    for s in range(SWEEPS):
        take_halo(s)

        def sweep(t, _, s=s):
            gather_rows(t, s)
            narrow_b(t)
            apply_faces(t)
            narrow_x(t)
            apply_inverse(t, s + 1)
            return 0

        lax.fori_loop(0, T, sweep, 0)
        if s + 1 < SWEEPS:
            send_halo(s + 1)
    out_ref[...] = adj[SWEEPS, :, 0:E]
    for s in range(SWEEPS):
        for d in range(6):

            @pl.when(sends[d])
            def _(s=s, d=d):
                halo_copy(s, d).wait_send()


def shards(inverse_blocks, face_blocks, load_vector, live_counts, nbr_kind, nbr_slot, send_x, send_yz):
    by_row = jnp.transpose(face_blocks, (1, 2, 0, 3))
    anywhere = pl.BlockSpec(memory_space=pl.ANY)
    on_core = pl.BlockSpec(memory_space=pltpu.VMEM)
    scalar = pl.BlockSpec(memory_space=pltpu.SMEM)
    result = pl.pallas_call(
        kernel,
        out_shape=jax.ShapeDtypeStruct((ROWS, E), BF),
        in_specs=[anywhere, anywhere, on_core, scalar, on_core, on_core, on_core, on_core],
        out_specs=on_core,
        scratch_shapes=[
            pltpu.VMEM((T, NB, FR, L), BF),
            pltpu.VMEM((T, NB // 2, 2 * XR, L), BF),
            pltpu.VMEM((SWEEPS + 1, ROWS, SRC), BF),
            pltpu.VMEM((T, NF * XS, L), F32),
            pltpu.VMEM((T, NF, 2 * XR, L), BF),
            pltpu.VMEM((T, NF * FS, L), F32),
            pltpu.VMEM((T, NF, FR, L), BF),
            pltpu.VMEM((E, HALO), BF),
            pltpu.VMEM((T, SRC, FACES * L), BF),
            pltpu.VMEM((SWEEPS, 2, ROWS, L), BF),
            pltpu.VMEM((SWEEPS, 4, PACK, L), BF),
            pltpu.VMEM((SWEEPS, 2, ROWS, L), BF),
            pltpu.VMEM((SWEEPS, 4, PACK, L), BF),
            pltpu.SemaphoreType.DMA((3 * T,)),
            pltpu.SemaphoreType.DMA((SWEEPS, 6)),
            pltpu.SemaphoreType.DMA((SWEEPS, 6)),
        ],
        compiler_params=pltpu.CompilerParams(
            vmem_limit_bytes=60 * 2**20, collective_id=0, has_side_effects=True
        ),
    )(
        inverse_blocks.reshape(NB // 2, 2, NB, E), by_row, load_vector.reshape(ROWS, E), live_counts,
        nbr_kind, nbr_slot, send_x, send_yz,
    )
    return result.reshape(NB, NF, E)


def solution(mesh):
    elements = ("gx", "gy", "gz")
    placed = (
        P(None, None, elements),
        P(None, None, None, elements),
        P(None, None, elements),
        P(elements),
        P(None, elements),
        P(None, elements),
        P(elements, None, None),
        P(elements, None, None),
    )
    return jax.shard_map(
        shards, mesh=mesh, in_specs=placed, out_specs=P(None, None, elements), check_vma=False
    )
```

```python
import jax
import jax.numpy as jnp
from jax import lax
from jax.experimental import pallas as pl
from jax.experimental.pallas import tpu as pltpu
from jax.sharding import PartitionSpec as P

BF = jnp.bfloat16
F32 = jnp.float32
I32 = jnp.int32
SWEEPS = 2
NB = 50
NF = 8
FACES = 4
HALVES = 2
KH = NF // HALVES
ROWS = NB * KH
E = 384
L = 128
T = E // L
FR = 208
FS = 216
XR = 56
XS = 72
HALO = 512
SRC = E + HALO
PACK = 104
DIRECTIONS = (("gx", 1), ("gx", -1), ("gy", 1), ("gy", -1), ("gz", 1), ("gz", -1))
OFFSETS = (0, E, E + 128, E + 256, E + 320, E + 384, E + 448)
MESH = pl.DeviceIdType.MESH
FACE_GROUPS = ((0, 1, 2), (3, 4, 5), (6, 7, 8), (9, 10, 11, 12))


def at16(index):
    return pl.ds(pl.multiple_of(index * 16, 16), 16)


def whole_tiles(get, count):
    value = jnp.concatenate([get(m) for m in range(count)], axis=0)
    return [value[16 * m : 16 * m + 16] for m in range(count)]


def added(terms):
    total = None
    for term in terms:
        total = term if total is None else total + term
    return total


def kernel(
    inv_hbm, face_hbm, load_ref, live_ref, kind_ref, slot_ref, sx_ref, syz_ref, out_ref,
    load_half, faces, inverse, adj, wide_x, vec_x, wide_b, vec_b, pick_send, pick, send_x, send_yz, recv_x, recv_yz,
    block_sem, send_sem, recv_sem,
):
    position = {axis: lax.axis_index(axis) for axis in ("gx", "gy", "gz")}
    sends, receives = [], []
    for axis, step in DIRECTIONS:
        length = lax.axis_size(axis)
        ahead, behind = position[axis] + step, position[axis] - step
        sends.append((ahead >= 0) & (ahead < length))
        receives.append((behind >= 0) & (behind < length))

    def block_copy(t, h):
        return pltpu.make_async_copy(
            inv_hbm.at[:, h, :, pl.ds(L * t, L)],
            inverse.at[t, :, pl.ds(XR * h, NB), :],
            block_sem.at[2 * t + h],
        )

    def face_copy(t):
        return pltpu.make_async_copy(
            face_hbm.reshape(NB, NB * FACES, E).at[:, :, pl.ds(L * t, L)],
            faces.at[t, :, pl.ds(0, NB * FACES), :],
            block_sem.at[2 * T + t],
        )

    def pad_row(i, _):
        for t in range(T):
            for h in range(2):
                inverse[t, i, XR * h + NB : XR * h + XR, :] = jnp.zeros((XR - NB, L), BF)
                faces[t, 2 * i + h, 200:208, :] = jnp.zeros((8, L), BF)
        return 0

    for t in range(T):
        for h in range(2):
            block_copy(t, h).start()
    for t in range(T):
        face_copy(t).start()

    lax.fori_loop(0, NB // 2, pad_row, 0, unroll=5)
    for t in range(T):
        for k in range(KH):
            wide_x[t, k * XS + 48 : k * XS + 56, :] = jnp.zeros((8, L), F32)
            wide_b[t, k * FS + 200 : k * FS + 208, :] = jnp.zeros((8, L), F32)

    for d in range(6):

        @pl.when(jnp.logical_not(receives[d]))
        def _(d=d):
            for p in range(SWEEPS * HALVES):
                if d < 2:
                    recv_x[p, d] = jnp.zeros((ROWS, L), BF)
                else:
                    recv_yz[p, d - 2] = jnp.zeros((PACK, L), BF)

    barrier = pltpu.get_barrier_semaphore()
    for d, (axis, step) in enumerate(DIRECTIONS):

        @pl.when(sends[d])
        def _(axis=axis, step=step):
            pl.semaphore_signal(
                barrier, inc=1, device_id={axis: position[axis] + step}, device_id_type=MESH
            )

    def halo_copy(s, h, d):
        p = HALVES * s + h
        axis, step = DIRECTIONS[d]
        source, target = (send_x, recv_x) if d < 2 else (send_yz, recv_yz)
        at = d if d < 2 else d - 2
        beside = jnp.clip(position[axis] + step, 0, lax.axis_size(axis) - 1)
        return pltpu.make_async_remote_copy(
            src_ref=source.at[p, at],
            dst_ref=target.at[p, at],
            send_sem=send_sem.at[p, d],
            recv_sem=recv_sem.at[p, d],
            device_id={axis: beside},
            device_id_type=MESH,
        )

    live = live_ref[...]
    lane = lax.broadcasted_iota(I32, (8, L), 1)
    low = lane < 64
    group_sum = (
        lax.shift_right_logical(lax.broadcasted_iota(I32, (8, L), 1), 4)
        == lax.broadcasted_iota(I32, (8, L), 0)
    )
    group_sum = group_sum.astype(F32).astype(BF)
    column = lax.broadcasted_iota(I32, (8, KH * 16), 1)
    split_sum = lax.shift_right_logical(column, 4) + lax.shift_right_logical(column & 8, 1)
    split_sum = split_sum == lax.broadcasted_iota(I32, (8, KH * 16), 0)
    split_sum = split_sum.astype(F32).astype(BF)

    def lanes(t):
        return pl.ds(pl.multiple_of(t * L, L), L)

    def scatter_x(t, i2, value):
        for half in range(2):
            wide_x[t, pl.ds(2 * i2 + half, KH, stride=XS), :] = value[KH * half : KH * half + KH]

    face_sum = jnp.concatenate([group_sum] * len(FACE_GROUPS), axis=1)
    inverse_sum = jnp.concatenate([group_sum, split_sum], axis=1)
    group2 = (
        lax.shift_right_logical(lax.broadcasted_iota(I32, (16, 256), 1), 4)
        == lax.broadcasted_iota(I32, (16, 256), 0)
    )
    group2 = group2.astype(F32).astype(BF)
    c2 = lax.broadcasted_iota(I32, (16, 2 * KH * 16), 1)
    b2 = lax.shift_right_logical(c2, 4)
    split2 = (b2 & 3) + lax.shift_left(b2 & 4, 1) + lax.shift_right_logical(c2 & 8, 1)
    split2 = split2 == lax.broadcasted_iota(I32, (16, 2 * KH * 16), 0)
    split2 = split2.astype(F32).astype(BF)
    face_sum2 = jnp.concatenate([group2] * len(FACE_GROUPS), axis=1)
    inverse_sum2 = jnp.concatenate([group2, split2], axis=1)

    def narrow_x(t):
        for k in range(KH):
            for m in range(2 * XR // 16):
                first = k * XS + (16 * m) % XR
                second = k * XS + (16 * m + 8) % XR
                both = jnp.concatenate(
                    [wide_x[t, first : first + 8, :], wide_x[t, second : second + 8, :]], axis=0
                )
                vec_x[t, k, 16 * m : 16 * m + 16, :] = both.astype(BF)

    def face_parts(t, i2):
        count = FR // 16
        tiles = [
            whole_tiles(lambda m, h=h: faces[t, 2 * i2 + h, 16 * m : 16 * m + 16, :], count)
            for h in range(2)
        ]
        sums = {}
        for k in range(KH):
            vector = whole_tiles(lambda m, k=k: vec_b[t, k, 16 * m : 16 * m + 16, :], count)
            for g, members in enumerate(FACE_GROUPS):
                for h in range(2):
                    sums[g, h, k] = added(tiles[h][m] * vector[m] for m in members)
        return [
            [sums[g, h, k] for h in range(2) for k in range(KH)] for g in range(len(FACE_GROUPS))
        ]

    def sum_faces(parts):
        stacked = [x for g in range(len(FACE_GROUPS)) for p in parts for x in p[g]]
        lhs = face_sum if len(parts) == 1 else face_sum2
        return jnp.dot(lhs, jnp.concatenate(stacked, axis=0), preferred_element_type=F32)

    def inverse_parts(t, i2):
        count = 2 * XR // 16
        tiles = whole_tiles(lambda m: inverse[t, i2, 16 * m : 16 * m + 16, :], count)
        sums = {}
        for k in range(KH):
            vector = whole_tiles(lambda m, k=k: vec_x[t, k, 16 * m : 16 * m + 16, :], count)
            products = [tiles[m] * vector[m] for m in range(count)]
            sums[0, k] = added(products[:3])
            sums[1, k] = added(products[4:])
            sums[2, k] = products[3]
        return [[sums[part, k] for part in (0, 1) for k in range(KH)], [sums[2, k] for k in range(KH)]]

    def sum_inverse(parts):
        stacked = [x for g in range(2) for p in parts for x in p[g]]
        lhs = inverse_sum if len(parts) == 1 else inverse_sum2
        return jnp.dot(lhs, jnp.concatenate(stacked, axis=0), preferred_element_type=F32)

    def rows_of_pairs():
        pairs = list(range(NB // 2))
        return [pairs[a : a + 2] for a in range(0, NB // 2, 2)]

    def split_load(t):
        for i2 in range(NB // 2):
            value = load_ref[16 * i2 : 16 * i2 + 16, lanes(t)].astype(F32)
            for h in range(HALVES):
                load_half[h, t, 8 * i2 : 8 * i2 + 8, :] = jnp.concatenate(
                    [value[KH * h : KH * h + KH], value[NF + KH * h : NF + KH * h + KH]], axis=0
                )

    def apply_inverse(t, s, h):
        alive = (lane + t * L) < live
        for group in rows_of_pairs():
            total = sum_inverse([inverse_parts(t, i2) for i2 in group])
            for n, i2 in enumerate(group):
                value = jnp.where(alive, total[8 * n : 8 * n + 8], 0.0)
                adj[s, h, 8 * i2 : 8 * i2 + 8, lanes(t)] = value.astype(BF)

    def apply_faces(t, h):
        for group in rows_of_pairs():
            total = sum_faces([face_parts(t, i2) for i2 in group])
            for n, i2 in enumerate(group):
                scatter_x(t, i2, load_half[h, t, 8 * i2 : 8 * i2 + 8, :] - total[8 * n : 8 * n + 8])

    lists = [sx_ref[0, 0:1, :], sx_ref[0, 1:2, :]]
    for pair in range(2):
        lists.append(
            jnp.concatenate(
                [syz_ref[0, 2 * pair : 2 * pair + 1, :], syz_ref[0, 2 * pair + 1 : 2 * pair + 2, :]],
                axis=1,
            )
        )
    for c in range(4):

        def fill_send(b, _, c=c):
            row = lax.broadcasted_iota(I32, (16, L), 0) + b * 16
            pick_send[at16(b), c * L : (c + 1) * L] = jnp.where(row == lists[c], 1.0, 0.0).astype(BF)
            return 0

        lax.fori_loop(0, E // 16, fill_send, 0, unroll=8)

    for t in range(T):
        for h in range(2):
            block_copy(t, h).wait()

    def first(h):
        def tile(t, _):
            if h == 0:
                split_load(t)
            for i2 in range(NB // 2):
                scatter_x(t, i2, load_half[h, t, 8 * i2 : 8 * i2 + 8, :])
            narrow_x(t)
            apply_inverse(t, 0, h)
            return 0

        lax.fori_loop(0, T, tile, 0)

    def send_halo(s, h):
        p = HALVES * s + h
        mine = adj[s, h, :, 0:E]
        four = jnp.dot(mine, pick_send[:, 2 * L : 4 * L], preferred_element_type=F32)
        for pair in (0, 1):
            both = four[:, pair * L : (pair + 1) * L]
            for r in range(PACK // 8):
                upper = both[8 * r : 8 * r + 8]
                if PACK + 8 * r < ROWS:
                    lower = both[PACK + 8 * r : PACK + 8 * r + 8]
                else:
                    lower = jnp.zeros((8, L), F32)
                ahead = jnp.where(low, upper, pltpu.roll(lower, 64, 1))
                behind = jnp.where(low, pltpu.roll(upper, 64, 1), lower)
                send_yz[p, 2 * pair, 8 * r : 8 * r + 8, :] = ahead.astype(BF)
                send_yz[p, 2 * pair + 1, 8 * r : 8 * r + 8, :] = behind.astype(BF)
        start_halo(s, h, (2, 3, 4, 5))
        two = jnp.dot(mine, pick_send[:, 0 : 2 * L], preferred_element_type=F32).astype(BF)
        for d in range(2):
            send_x[p, d] = two[:, d * L : (d + 1) * L]
        start_halo(s, h, (0, 1))

    def start_halo(s, h, directions):
        for d in directions:

            @pl.when(sends[d])
            def _(d=d):
                halo_copy(s, h, d).start()

    def take_halo(s, h):
        p = HALVES * s + h
        for d in range(6):

            @pl.when(receives[d])
            def _(d=d):
                halo_copy(s, h, d).wait_recv()

        for d in range(2):
            adj[s, h, :, E + d * L : E + (d + 1) * L] = recv_x[p, d]
        for pair in range(2):
            column = E + (2 + pair) * L
            for r in range(PACK // 8):
                ahead = recv_yz[p, 2 * pair, 8 * r : 8 * r + 8, :].astype(F32)
                behind = recv_yz[p, 2 * pair + 1, 8 * r : 8 * r + 8, :].astype(F32)
                upper = jnp.where(low, ahead, pltpu.roll(behind, 64, 1))
                adj[s, h, 8 * r : 8 * r + 8, column : column + L] = upper.astype(BF)
                if PACK + 8 * r < ROWS:
                    lower = jnp.where(low, pltpu.roll(ahead, 64, 1), behind)
                    adj[s, h, PACK + 8 * r : PACK + 8 * r + 8, column : column + L] = lower.astype(BF)

    def gather_rows(t, s, h):
        for f in range(0, FACES, 2):
            picked = jnp.dot(adj[s, h], pick[t, :, f * L : (f + 2) * L], preferred_element_type=F32)
            for j in range(NB):
                for g in range(2):
                    rows = pl.ds(FACES * j + f + g, KH, stride=FS)
                    wide_b[t, rows, :] = picked[KH * j : KH * j + KH, g * L : (g + 1) * L]

    def narrow_b(t):
        for k in range(KH):
            for m in range(FR // 16):
                r = k * FS + 16 * m
                vec_b[t, k, 16 * m : 16 * m + 16, :] = wide_b[t, r : r + 16, :].astype(BF)

    first(0)
    pl.semaphore_wait(barrier, sum(jnp.where(there, 1, 0) for there in sends))
    send_halo(0, 0)
    first(1)
    send_halo(0, 1)

    kind = kind_ref[...]
    look = jnp.where(kind == 0, -1, slot_ref[...])
    for d in range(7):
        look = look + jnp.where(kind == d + 1, OFFSETS[d], 0)
    for t in range(T):
        for f in range(FACES):
            wanted = look[f : f + 1, t * L : (t + 1) * L]

            def fill(b, _, t=t, f=f, wanted=wanted):
                row = lax.broadcasted_iota(I32, (16, L), 0) + b * 16
                pick[t, at16(b), f * L : (f + 1) * L] = jnp.where(row == wanted, 1.0, 0.0).astype(BF)
                return 0

            lax.fori_loop(0, SRC // 16, fill, 0, unroll=8)
    for t in range(T):
        face_copy(t).wait()

    for s in range(SWEEPS):
        for h in range(HALVES):
            take_halo(s, h)

            def sweep(t, _, s=s, h=h):
                gather_rows(t, s, h)
                narrow_b(t)
                apply_faces(t, h)
                narrow_x(t)
                apply_inverse(t, s + 1, h)
                return 0

            lax.fori_loop(0, T, sweep, 0)
            if s + 1 < SWEEPS:
                send_halo(s + 1, h)

    def join(t, _):
        for i2 in range(NB // 2):
            one, two = (adj[SWEEPS, h, 8 * i2 : 8 * i2 + 8, lanes(t)].astype(F32) for h in range(HALVES))
            value = jnp.concatenate([one[:KH], two[:KH], one[KH:], two[KH:]], axis=0)
            out_ref[16 * i2 : 16 * i2 + 16, lanes(t)] = value.astype(BF)
        return 0

    lax.fori_loop(0, T, join, 0)
    for s in range(SWEEPS):
        for h in range(HALVES):
            for d in range(6):

                @pl.when(sends[d])
                def _(s=s, h=h, d=d):
                    halo_copy(s, h, d).wait_send()


def shards(inverse_blocks, face_blocks, load_vector, live_counts, nbr_kind, nbr_slot, send_x, send_yz):
    by_row = jnp.transpose(face_blocks, (1, 2, 0, 3))
    anywhere = pl.BlockSpec(memory_space=pl.ANY)
    on_core = pl.BlockSpec(memory_space=pltpu.VMEM)
    result = pl.pallas_call(
        kernel,
        out_shape=jax.ShapeDtypeStruct((NB * NF, E), BF),
        in_specs=[anywhere, anywhere, on_core, on_core, on_core, on_core, on_core, on_core],
        out_specs=on_core,
        scratch_shapes=[
            pltpu.VMEM((HALVES, T, ROWS, L), F32),
            pltpu.VMEM((T, NB, FR, L), BF),
            pltpu.VMEM((T, NB // 2, 2 * XR, L), BF),
            pltpu.VMEM((SWEEPS + 1, HALVES, ROWS, SRC), BF),
            pltpu.VMEM((T, KH * XS, L), F32),
            pltpu.VMEM((T, KH, 2 * XR, L), BF),
            pltpu.VMEM((T, KH * FS, L), F32),
            pltpu.VMEM((T, KH, FR, L), BF),
            pltpu.VMEM((E, HALO), BF),
            pltpu.VMEM((T, SRC, FACES * L), BF),
            pltpu.VMEM((SWEEPS * HALVES, 2, ROWS, L), BF),
            pltpu.VMEM((SWEEPS * HALVES, 4, PACK, L), BF),
            pltpu.VMEM((SWEEPS * HALVES, 2, ROWS, L), BF),
            pltpu.VMEM((SWEEPS * HALVES, 4, PACK, L), BF),
            pltpu.SemaphoreType.DMA((3 * T,)),
            pltpu.SemaphoreType.DMA((SWEEPS * HALVES, 6)),
            pltpu.SemaphoreType.DMA((SWEEPS * HALVES, 6)),
        ],
        compiler_params=pltpu.CompilerParams(
            vmem_limit_bytes=60 * 2**20, collective_id=0, has_side_effects=True
        ),
    )(
        inverse_blocks.reshape(NB // 2, 2, NB, E), by_row, load_vector.reshape(NB * NF, E), live_counts.reshape(1, 1),
        nbr_kind, nbr_slot, send_x, send_yz,
    )
    return result.reshape(NB, NF, E)


def solution(mesh):
    elements = ("gx", "gy", "gz")
    placed = (
        P(None, None, elements),
        P(None, None, None, elements),
        P(None, None, elements),
        P(elements),
        P(None, elements),
        P(None, elements),
        P(elements, None, None),
        P(elements, None, None),
    )
    return jax.shard_map(
        shards, mesh=mesh, in_specs=placed, out_specs=P(None, None, elements), check_vma=False
    )
```
